32 devices in a mesh: section: 2 (over core), seq: 4 (over z), fsdp: 4 (over y, x).
Axes of the slice: x: 2, y: 2, z: 4, core: 2. Of those that a mesh axis runs over, the one named last changes fastest.
Arguments:
- inputs: bfloat16 [4, 4, 512, 1024], P(None, 'fsdp', 'seq'), may hold values from -6 to 6
- cotangent: bfloat16 [4, 4, 512, 1024], P(None, 'fsdp', 'seq'), may hold values from -6 to 6
- doc_lengths: int32 [4, 4, 4], P(None, 'fsdp'), may hold values from 1 to 256, 512 in all within a row
- qkv_weight: bfloat16 [2, 1024, 3072], P('section', ('seq', 'fsdp')), may hold values from -0.1875 to 0.1875
- out_weight: bfloat16 [2, 1024, 1024], P('section', ('seq', 'fsdp')), may hold values from -1.5 to 1.5
- attn_gain: bfloat16 [2, 1024], P('section', ('seq', 'fsdp')), may hold values from 0.5 to 1.5
- wide_weight: bfloat16 [2, 1024, 5248], P('section', ('seq', 'fsdp')), may hold values from -0.1875 to 0.1875
- narrow_weight: bfloat16 [2, 1024, 2624], P('section', ('seq', 'fsdp')), may hold values from -0.125 to 0.125
- mlp_gain: bfloat16 [2, 1024], P('section', ('seq', 'fsdp')), may hold values from 0.5 to 1.5
Outputs:
- activations: bfloat16 [2, 4, 4, 512, 1024], P('section', None, 'fsdp', 'seq')
- input_grads: float32 [2, 4, 4, 512, 1024], P('section', None, 'fsdp', 'seq')
- qkv_grad: float32 [2, 1024, 3072], P('section', ('seq', 'fsdp'))
- out_grad: float32 [2, 1024, 1024], P('section', ('seq', 'fsdp'))
- attn_gain_grad: float32 [2, 1024], P('section', ('seq', 'fsdp'))
- wide_grad: float32 [2, 1024, 5248], P('section', ('seq', 'fsdp'))
- narrow_grad: float32 [2, 1024, 2624], P('section', ('seq', 'fsdp'))
- mlp_gain_grad: float32 [2, 1024], P('section', ('seq', 'fsdp'))
The draws below stay inside these ranges and needn't reach their ends.
Inputs may be any that keep to these rules, and one draw needn't show every extreme that they name: `doc_lengths`: the 4 entries of a sequence are its documents' lengths in order; they sum to 512, and in every sequence the longest is exactly 256.
All inputs are finite; a program needn't handle non-finite values.
Results may differ from the reference program's by a relative error of at most 0.023.
Values may be sent and summed in bfloat16 or wider, within the bound.
No kernel may reach another device: no remote copies, remote signals or barrier semaphores. Data moves between devices by JAX's collectives and lax.ppermute only.
A program may use at most 320 MiB of HBM per device.

```python
import math
import jax
import jax.numpy as jnp
import numpy as np
from jax import lax

D = 1024
FF = 2624
HEADS = 16
HEAD_DIM = 64
HALF = 64
MICRO = 4
DOCS = 4
SECTIONS = 2
SEQS = 4
LEN = 512
DOC_MOST = 256


def with_spikes(values, rng, source, target, parts, factor):
    owner, partner = [(jnp.arange(values.shape[position]) // (values.shape[position] // parts)).reshape([-1 if axis == position else 1 for axis in range(values.ndim)]) for position in (source, target)]
    chosen = jax.random.permutation(rng, parts)[partner]
    strong = (owner == chosen) | (owner == (partner + parts // 2) % parts)
    return jnp.where(strong, factor * values, values)


def levels(stream_key, extent, split, low, top_value):
    loudness, own = 1.0, jax.random.fold_in(stream_key, 6)
    for dim, shards_of in split:
        steps = jnp.exp(jax.random.uniform(jax.random.fold_in(own, dim), (shards_of,), jnp.float32, low / len(split), top_value / len(split)))
        loudness = loudness * jnp.repeat(steps, extent[dim] // shards_of).reshape([-1 if axis == dim else 1 for axis in range(len(extent))])
    return loudness


def profile(number_of, total, limit, skew):
    portions = [(1 << 20) // math.isqrt(rank ** skew) + 1 for rank in range(2, number_of + 1)]
    rest, holding = total - limit - (number_of - 1), [1] * (number_of - 1)
    while rest > 0:
        free = [i for i in range(number_of - 1) if holding[i] < limit]
        pool, budget = sum([portions[i] for i in free]), rest
        for i in free:
            extra = min(limit - holding[i], max(1, budget * portions[i] // pool), rest)
            holding[i] = holding[i] + extra
            rest = rest - extra
    return np.array([limit] + holding)


def ragged(own_key, count, total, reach, skew):
    if count == 2:
        one = jax.random.randint(own_key, (), max(1, total - reach), min(reach, total - 1) + 1)
        return jnp.stack([one, total - one])
    tallies = jnp.asarray(profile(count, total, reach, skew), jnp.int32)
    twos = (count - 1) // 2
    giver, taker = tallies[1:1 + 2 * twos:2], tallies[2:2 + 2 * twos:2]
    margin = jnp.minimum(giver - 1, reach - taker)
    moved = jax.random.randint(jax.random.fold_in(own_key, 1), (twos,), 0, 1 << 20) % (margin + 1)
    tallies = tallies.at[1:1 + 2 * twos:2].set(giver - moved).at[2:2 + 2 * twos:2].set(taker + moved)
    return tallies[jax.random.permutation(jax.random.fold_in(own_key, 2), count)]


def gaussian(stream_key, shape, scale, reach, cuts=(), dtype=jnp.bfloat16):
    array = jax.random.normal(stream_key, shape, jnp.float32) * scale
    if len(cuts) > 0:
        array = levels(stream_key, shape, cuts, -0.22, 0.18) * array
    return jnp.clip(array, min=-reach, max=reach).astype(dtype)


def gaussian_with(stream_key, dims, scale, most, cuts, heavy, kind=jnp.bfloat16):
    entries = scale * jax.random.normal(stream_key, dims, jnp.float32)
    if cuts:
        entries = entries * levels(stream_key, dims, cuts, -0.22, 0.18)
    return jnp.clip(with_spikes(entries, jax.random.fold_in(stream_key, 3), *heavy), -most, most).astype(kind)


def setup_inputs(seed: int = 0) -> dict:
    splits = jax.random.split(jax.random.key(seed), 10)
    inputs = gaussian(splits[0], (MICRO, SEQS, LEN, D), 1.0, 6.0, ((1, 4), (2, 4)))
    cotangent = gaussian_with(splits[1], (MICRO, SEQS, LEN, D), 1.0, 6.0, ((1, 4), (2, 4)), (2, 3, 4, 2.0))
    doc_lengths = jax.vmap(lambda own: ragged(own, DOCS, LEN, DOC_MOST, 2))(jax.random.split(splits[2], MICRO * SEQS)).reshape((MICRO, SEQS, DOCS)).astype(jnp.int32)
    qkv_weight = gaussian(splits[3], (SECTIONS, D, 3 * D), D ** -0.5, 0.1875, ((0, 2), (1, 16)))
    out_weight = gaussian(splits[4], (SECTIONS, D, D), (D // HALF) ** -0.5, 1.5, ((0, 2), (1, 16)))
    attn_gain = jnp.clip(1.0 + 0.1 * jax.random.normal(splits[5], (SECTIONS, D), jnp.float32), 0.5, 1.5).astype(jnp.bfloat16)
    wide_weight = gaussian(splits[6], (SECTIONS, D, 2 * FF), D ** -0.5, 0.1875, ((0, 2), (1, 16)))
    narrow_weight = gaussian(splits[7], (SECTIONS, D, FF), FF ** -0.5, 0.125, ((0, 2), (1, 16)))
    mlp_gain = jnp.clip(1.0 + 0.1 * jax.random.normal(splits[8], (SECTIONS, D), jnp.float32), 0.5, 1.5).astype(jnp.bfloat16)
    return {"inputs": inputs, "cotangent": cotangent, "doc_lengths": doc_lengths, "qkv_weight": qkv_weight, "out_weight": out_weight, "attn_gain": attn_gain, "wide_weight": wide_weight, "narrow_weight": narrow_weight, "mlp_gain": mlp_gain}


@jax.custom_vjp
def low(v):
    return lax.optimization_barrier(v.astype(jnp.bfloat16)).astype(jnp.float32)

@jax.custom_vjp
def low_back(v):
    return v

def low_keep(v):
    return (low(v), None)

def low_pass(kept, grad):
    return (grad,)

def back_keep(v):
    return (v, None)

def back_low(kept, grad):
    return (low(grad),)
low.defvjp(low_keep, low_pass)
low_back.defvjp(back_keep, back_low)
eps_norm = 1e-05
theta_base = 10000.0
masked_fill = -1e+30

def matmul(left, right):
    return jnp.dot(left, right, precision=lax.Precision.HIGHEST, preferred_element_type=jnp.float32)

def layer_norm(values, gain):
    center = lax.optimization_barrier(jnp.mean(values, axis=-1, keepdims=True))
    shifted = values - center
    spread = lax.optimization_barrier(jnp.mean(shifted * shifted, axis=-1, keepdims=True))
    return shifted * lax.rsqrt(spread + eps_norm) * gain

def rotate(values, cosine, sine_table):
    half_dim = values.shape[-1] // 2
    first_half = values[..., :half_dim]
    second_half = values[..., half_dim:]
    return jnp.concatenate([first_half * cosine - second_half * sine_table, second_half * cosine + first_half * sine_table], axis=-1)

def rotary_tables():
    half_dim = HEAD_DIM // 2
    frequency = jnp.power(theta_base, jnp.arange(half_dim).astype(jnp.float32) * (-2.0 / HEAD_DIM))
    angles = jnp.arange(LEN).astype(jnp.float32)[:, None] * frequency[None, :]
    return (jnp.cos(angles)[:, None, :], jnp.sin(angles)[:, None, :])

def attend(queries, keys, values, documents):
    block = min(512, LEN)
    count = LEN // block
    pad_spec = ((HALF, HALF), (0, 0), (0, 0))
    keys_pad = jnp.pad(keys, pad_spec)
    values_pad = jnp.pad(values, pad_spec)
    docs_pad = jnp.pad(documents, (HALF, HALF), constant_values=-1)
    score_scale = HEAD_DIM ** (-0.5)
    width_keys = block + 2 * HALF
    nearby = jnp.abs(jnp.arange(block)[:, None] - jnp.arange(width_keys)[None, :] + HALF) <= HALF

    def one_block(index):
        start = (index * block).astype(jnp.int32)
        q_block = lax.dynamic_slice_in_dim(queries, start, block, 0)
        k_block = lax.dynamic_slice_in_dim(keys_pad, start, width_keys, 0)
        v_block = lax.dynamic_slice_in_dim(values_pad, start, width_keys, 0)
        doc_rows = lax.dynamic_slice_in_dim(documents, start, block, 0)
        doc_cols = lax.dynamic_slice_in_dim(docs_pad, start, width_keys, 0)
        allowed = nearby & (doc_rows[:, None] == doc_cols[None, :])
        scores = jnp.einsum('qhd,khd->hqk', q_block, k_block, precision=lax.Precision.HIGHEST) * score_scale
        scores = jnp.where(allowed[None], low_back(scores), masked_fill)
        row_peak = lax.optimization_barrier(jnp.max(scores, axis=-1, keepdims=True))
        exp_scores = jnp.exp(scores - row_peak)
        softmax_prob = exp_scores / lax.optimization_barrier(jnp.sum(exp_scores, axis=-1, keepdims=True))
        return jnp.einsum('hqk,khd->qhd', low(softmax_prob), v_block, precision=lax.Precision.HIGHEST)
    blocks = lax.map(jax.checkpoint(one_block), jnp.arange(count).astype(jnp.int32))
    return blocks.reshape(LEN, HEADS * HEAD_DIM)

def layer(hidden, weights, documents, cosine, sine_table):
    qkv_w, out_w, wide_w, narrow_w, attn_g, mlp_g = weights
    normed = low(layer_norm(hidden, attn_g))
    mixed = matmul(normed, qkv_w)
    head_shape = (LEN, HEADS, HEAD_DIM)
    queries = low(rotate(low_back(mixed[:, :D]).reshape(head_shape), cosine, sine_table))
    keys = low(rotate(low_back(mixed[:, D:2 * D]).reshape(head_shape), cosine, sine_table))
    values = low(low_back(mixed[:, 2 * D:])).reshape(head_shape)
    attended = low(low_back(attend(queries, keys, values, documents)))
    middle = hidden + low_back(matmul(attended, out_w))
    normed_mlp = low(layer_norm(middle, mlp_g))
    wide = low_back(matmul(normed_mlp, wide_w))
    product = low(jax.nn.gelu(wide[:, :FF], approximate=False) * wide[:, FF:])
    return middle + low_back(matmul(product, narrow_w.T))

def reference(inputs, cotangent, doc_lengths, qkv_weight, out_weight, attn_gain, wide_weight, narrow_weight, mlp_gain):
    weights = tuple((weight.astype(jnp.float32) for weight in (qkv_weight, out_weight, wide_weight, narrow_weight, attn_gain, mlp_gain)))
    cosine, sine_table = rotary_tables()
    seq_count = MICRO * SEQS
    seq_inputs = inputs.reshape(seq_count, LEN, D).astype(jnp.float32)
    seq_cot = cotangent.reshape(seq_count, LEN, D).astype(jnp.float32)
    seq_lengths = doc_lengths.reshape(seq_count, DOCS).astype(jnp.int32)
    positions = jnp.arange(LEN).astype(jnp.int32)

    def one_sequence(totals, pieces):
        start_in, cot_in, lengths_row = pieces
        ends = jnp.cumsum(lengths_row).astype(jnp.int32)
        documents = lax.optimization_barrier(jnp.sum((ends[None, :] <= positions[:, None]).astype(jnp.int32), axis=1)).astype(jnp.int32)

        def forward(layer_params, offsets):
            current = start_in + offsets[0]
            outputs = []
            for layer_num in range(SECTIONS):
                if layer_num > 0:
                    current = low(low_back(outputs[-1])) + offsets[layer_num]
                chosen = tuple((weight[layer_num] for weight in layer_params))
                outputs.append(layer(current, chosen, documents, cosine, sine_table))
            loss_value = jnp.sum(outputs[-1] * cot_in)
            return (loss_value, jnp.stack(outputs))
        offsets = jnp.zeros((SECTIONS, LEN, D), jnp.float32)
        loss_value, pullback, outputs = jax.vjp(forward, weights, offsets, has_aux=True)
        weight_grads, input_grads = pullback(jnp.ones_like(loss_value))
        totals = jax.tree.map(lambda summed, added: summed + added, totals, weight_grads)
        return (totals, (outputs.astype(jnp.bfloat16), input_grads))
    zeros_init = tuple((jnp.zeros_like(weight) for weight in weights))
    totals, (acts, grads_in) = lax.scan(one_sequence, zeros_init, (seq_inputs, seq_cot, seq_lengths))
    activations = jnp.transpose(acts.reshape(MICRO, SEQS, SECTIONS, LEN, D), (2, 0, 1, 3, 4))
    input_grads = jnp.transpose(grads_in.reshape(MICRO, SEQS, SECTIONS, LEN, D), (2, 0, 1, 3, 4))
    return (activations, input_grads, totals[0], totals[1], totals[4], totals[2], totals[3], totals[5])
```

```python
import math

import jax
import jax.numpy as jnp
from jax import lax
from jax.sharding import PartitionSpec as P

D = 1024
FF = 2624
HEADS = 16
HEAD_DIM = 64
HALF = 64


eps_norm = 1e-05
theta_base = 10000.0
masked_fill = -1e30


def norm_forward(values):
    center = jnp.mean(values, axis=-1, keepdims=True)
    shifted = values - center
    spread = jnp.mean(shifted * shifted, axis=-1, keepdims=True)
    inverse = lax.rsqrt(spread + eps_norm)
    return (shifted * inverse, inverse)


def norm_backward(grad_out, normed, inverse, gain):
    scaled = grad_out * gain
    gain_grad = jnp.sum(grad_out * normed, axis=0)
    first_mean = jnp.mean(scaled, axis=-1, keepdims=True)
    second_mean = jnp.mean(scaled * normed, axis=-1, keepdims=True)
    return (inverse * (scaled - first_mean - normed * second_mean), gain_grad)


def rotate(values, cosine, sine_table):
    half_dim = values.shape[-1] // 2
    first_half = values[..., :half_dim]
    second_half = values[..., half_dim:]
    return jnp.concatenate(
        [
            first_half * cosine - second_half * sine_table,
            second_half * cosine + first_half * sine_table,
        ],
        axis=-1,
    )


def rotate_back(grads, cosine, sine_table):
    half_dim = grads.shape[-1] // 2
    first_half = grads[..., :half_dim]
    second_half = grads[..., half_dim:]
    return jnp.concatenate(
        [
            first_half * cosine + second_half * sine_table,
            second_half * cosine - first_half * sine_table,
        ],
        axis=-1,
    )


def gelu_slope(values):
    normal_cdf = 0.5 * (1.0 + jax.scipy.special.erf(values * 2.0 ** (-0.5)))
    return normal_cdf + values * jnp.exp(-0.5 * values * values) * (2.0 * math.pi) ** (-0.5)


def make_tables(lengths_row, seq_num, tokens_here, total_len):
    ends = jnp.cumsum(lengths_row)
    spots = seq_num * tokens_here - HALF + jnp.arange(tokens_here + 2 * HALF, dtype=jnp.int32)
    doc_ext = jnp.sum((ends[None, :] <= spots[:, None]).astype(jnp.int32), axis=1)
    inside = (spots >= 0) & (spots < total_len)
    doc_rows = doc_ext[HALF : HALF + tokens_here]
    nearby = (
        jnp.abs(
            jnp.arange(tokens_here)[:, None] - jnp.arange(tokens_here + 2 * HALF)[None, :] + HALF
        )
        <= HALF
    )
    return nearby & inside[None, :] & (doc_rows[:, None] == doc_ext[None, :])


def flip_pairs(order, spots):
    pairs = []
    for section in range(2):
        bit = (1, 2)[(section + order) % 2]
        pairs += [(section * spots + spot, section * spots + (spot ^ bit)) for spot in range(spots)]
    return pairs


def flip(x, order):
    return lax.ppermute(x, ("section", "fsdp"), flip_pairs(order, lax.axis_size("fsdp")))


def swap_cores(x):
    return lax.ppermute(x, "section", [(0, 1), (1, 0)])


def shift_seq(x, by):
    count = lax.axis_size("seq")
    return lax.ppermute(x, "seq", [(i, (i + by) % count) for i in range(count)])


def halo(block, width):
    count = lax.axis_size("seq")
    forward = [(i, i + 1) for i in range(count - 1)]
    backward = [(target, source) for source, target in forward]
    low = lax.ppermute(block[:, block.shape[1] - width :], "seq", forward)
    high = lax.ppermute(block[:, :width], "seq", backward)
    return low, high


def own_halves(shard, core):
    rows = shard.shape[0] // 2
    mine = lax.dynamic_slice_in_dim(shard, core * rows, rows, 0)
    received = swap_cores(lax.dynamic_slice_in_dim(shard, (1 - core) * rows, rows, 0))
    return [jnp.where(core == layer, mine, received) for layer in range(2)]


def along_seq(half):
    count, place = lax.axis_size("seq"), lax.axis_index("seq")
    out = jnp.zeros((count,) + half.shape, half.dtype)
    out = lax.dynamic_update_slice(out, half[None], (place, 0, 0))
    for by in range(1, count):
        out = lax.dynamic_update_slice(out, shift_seq(half, by)[None], ((place - by) % count, 0, 0))
    return out


def gather_rest(column, core):
    spots, spot = lax.axis_size("fsdp"), lax.axis_index("fsdp")
    seq_count, rows, columns = column.shape
    first_bit = jnp.where(core == 0, 1, 2)
    other_bit = 3 - first_bit
    full = jnp.zeros((seq_count, spots * 2, rows, columns), column.dtype)

    def put(full, piece, place, half):
        return lax.dynamic_update_slice(full, piece[:, None], (0, place * 2 + half, 0, 0))

    one = flip(column, 0)
    two = flip(column, 1)
    three = flip(one, 1)
    for piece, place, swapped in (
        (column, spot, spot),
        (one, spot ^ first_bit, spot ^ other_bit),
        (two, spot ^ other_bit, spot ^ first_bit),
        (three, spot ^ 3, spot ^ 3),
    ):
        full = put(full, piece, place, core)
        full = put(full, swap_cores(piece), swapped, 1 - core)
    return full.reshape(seq_count * spots * 2 * rows, columns)


def weight_grad(left, right, core):
    seq_count, place = lax.axis_size("seq"), lax.axis_index("seq")
    spots, spot = lax.axis_size("fsdp"), lax.axis_index("fsdp")
    tokens, width = left.shape
    columns = right.shape[1]
    rows = width // (seq_count * spots * 2)
    first_bit = jnp.where(core == 0, 1, 2)
    other_bit = 3 - first_bit
    turned = left.T.reshape(seq_count, spots * 2, rows, tokens)

    def product(places, half):
        chosen = [lax.dynamic_slice_in_dim(turned, p * 2 + half, 1, 1)[:, 0] for p in places]
        chosen = jnp.stack(chosen).reshape(len(places) * seq_count * rows, tokens)
        out = jnp.dot(chosen, right, preferred_element_type=jnp.float32).astype(jnp.bfloat16)
        return out.reshape(len(places), seq_count, rows, columns)

    wide = lambda value: value.astype(jnp.float32)
    low = lambda value: value.astype(jnp.bfloat16)
    sent = swap_cores(product((spot ^ other_bit, spot ^ 3), 1 - core))
    kept = swap_cores(product((spot, spot ^ first_bit), 1 - core))
    one = flip(low(wide(product((spot ^ first_bit, spot ^ 3), core)) + wide(sent)), 0)
    base = product((spot, spot ^ other_bit), core)
    two = flip(low(wide(base[1]) + wide(kept[1]) + wide(one[1])), 1)
    mine = low(wide(base[0]) + wide(kept[0]) + wide(one[0]) + wide(two))
    total = wide(lax.dynamic_index_in_dim(mine, place, 0, keepdims=False))
    for by in range(1, seq_count):
        out = lax.dynamic_index_in_dim(mine, (place + by) % seq_count, 0, keepdims=False)
        total = total + wide(shift_seq(out, by))
    return total


def owner_rows(pieces, core):
    mine = jnp.where(core == 0, pieces[0], pieces[1])
    received = swap_cores(jnp.where(core == 0, pieces[1], pieces[0]))
    first = core == 0
    return jnp.concatenate(
        [jnp.where(first, mine, received), jnp.where(first, received, mine)], axis=0
    )


def sum_everywhere(x):
    x = x + swap_cores(x)
    x = x + flip(x, 0)
    x = x + flip(x, 1)
    return x + sum(shift_seq(x, by) for by in range(1, lax.axis_size("seq")))


def forward_layer(hidden, params, allowed, cosine, sine_table):
    w_mix, w_mlp, gain_attn, gain_mlp = params
    batch, tokens = allowed.shape[:2]
    score_scale = HEAD_DIM ** (-0.5)
    normed_a, inverse_a = norm_forward(hidden)
    a_low = (normed_a * gain_attn).astype(jnp.bfloat16)
    mixed = jnp.dot(a_low, w_mix[:, : 3 * D], preferred_element_type=jnp.float32)
    head_shape = (batch, tokens, HEADS, HEAD_DIM)
    queries = rotate(mixed[:, :D].reshape(head_shape), cosine, sine_table).astype(jnp.bfloat16)
    keys = rotate(mixed[:, D : 2 * D].reshape(head_shape), cosine, sine_table).astype(jnp.bfloat16)
    values = mixed[:, 2 * D :].astype(jnp.bfloat16)
    key_value = jnp.concatenate(
        [keys.reshape(batch, tokens, D), values.reshape(batch, tokens, D)], axis=2
    )
    low, high = halo(key_value, HALF)
    kv_ext = jnp.concatenate([low, key_value, high], axis=1)
    ext_shape = (batch, tokens + 2 * HALF, HEADS, HEAD_DIM)
    k_ext = kv_ext[..., :D].reshape(ext_shape)
    v_ext = kv_ext[..., D:].reshape(ext_shape)
    scores = (
        jnp.einsum("bqhd,bkhd->bhqk", queries, k_ext, preferred_element_type=jnp.float32)
        * score_scale
    )
    scores = jnp.where(allowed[:, None], scores, masked_fill)
    row_peak = jnp.max(scores, axis=-1, keepdims=True)
    exp_scores = jnp.exp(scores - row_peak)
    softmax_prob = exp_scores / jnp.sum(exp_scores, axis=-1, keepdims=True)
    attended = jnp.einsum(
        "bhqk,bkhd->bqhd",
        softmax_prob.astype(jnp.bfloat16),
        v_ext,
        preferred_element_type=jnp.float32,
    )
    o_low = attended.reshape(batch * tokens, D).astype(jnp.bfloat16)
    middle = hidden + jnp.dot(o_low, w_mix[:, 3 * D : 4 * D], preferred_element_type=jnp.float32)
    normed_b, inverse_b = norm_forward(middle)
    b_low = (normed_b * gain_mlp).astype(jnp.bfloat16)
    wide = jnp.dot(b_low, w_mlp[:, : 2 * FF], preferred_element_type=jnp.float32)
    m_low = (jax.nn.gelu(wide[:, :FF], approximate=False) * wide[:, FF:]).astype(jnp.bfloat16)
    output = middle + jnp.einsum(
        "tf,df->td", m_low, w_mlp[:, 2 * FF :], preferred_element_type=jnp.float32
    )
    saved = (hidden, a_low, queries, k_ext, v_ext, softmax_prob, o_low, middle, b_low, wide, m_low)
    return (output, saved)


def backward_mlp(grad_out, saved, params, core):
    w_mix, w_mlp, gain_attn, gain_mlp = params
    hidden, a_low, queries, k_ext, v_ext, softmax_prob, o_low, middle, b_low, wide, m_low = saved
    g_mlp = grad_out.astype(jnp.bfloat16)
    grad_narrow = weight_grad(g_mlp, m_low, core)
    grad_m = jnp.dot(g_mlp, w_mlp[:, 2 * FF :], preferred_element_type=jnp.float32)
    gelu_input = wide[:, :FF]
    gate_part = wide[:, FF:]
    activated = jax.nn.gelu(gelu_input, approximate=False)
    grad_wide = jnp.concatenate(
        [grad_m * gate_part * gelu_slope(gelu_input), grad_m * activated], axis=1
    ).astype(jnp.bfloat16)
    grad_w_wide = weight_grad(b_low, grad_wide, core)
    grad_b = jnp.einsum(
        "tf,df->td", grad_wide, w_mlp[:, : 2 * FF], preferred_element_type=jnp.float32
    )
    normed_b, inverse_b = norm_forward(middle)
    grad_mid_part, grad_gain_mlp = norm_backward(grad_b, normed_b, inverse_b, gain_mlp)
    return (grad_out + grad_mid_part, (grad_w_wide, grad_narrow, grad_gain_mlp))


def backward_attn(grad_middle, saved, params, core, cosine, sine_table):
    w_mix, w_mlp, gain_attn, gain_mlp = params
    hidden, a_low, queries, k_ext, v_ext, softmax_prob, o_low, middle, b_low, wide, m_low = saved
    batch, tokens = queries.shape[:2]
    ext_rows = k_ext.shape[1]
    score_scale = HEAD_DIM ** (-0.5)
    g_attn = grad_middle.astype(jnp.bfloat16)
    grad_w_out = weight_grad(o_low, g_attn, core)
    grad_o = jnp.einsum(
        "te,de->td", g_attn, w_mix[:, 3 * D : 4 * D], preferred_element_type=jnp.float32
    ).astype(jnp.bfloat16)
    head_shape = (batch, tokens, HEADS, HEAD_DIM)
    grad_o = grad_o.reshape(head_shape)
    grad_prob = jnp.einsum("bqhd,bkhd->bhqk", grad_o, v_ext, preferred_element_type=jnp.float32)
    grad_v_ext = jnp.einsum(
        "bhqk,bqhd->bkhd",
        softmax_prob.astype(jnp.bfloat16),
        grad_o,
        preferred_element_type=jnp.float32,
    )
    row_delta = jnp.sum(softmax_prob * grad_prob, axis=-1, keepdims=True)
    grad_scores = (softmax_prob * (grad_prob - row_delta)).astype(jnp.bfloat16)
    grad_q = (
        jnp.einsum("bhqk,bkhd->bqhd", grad_scores, k_ext, preferred_element_type=jnp.float32)
        * score_scale
    )
    grad_k_ext = (
        jnp.einsum("bhqk,bqhd->bkhd", grad_scores, queries, preferred_element_type=jnp.float32)
        * score_scale
    )
    grad_kv_ext = jnp.concatenate(
        [grad_k_ext.reshape(batch, ext_rows, D), grad_v_ext.reshape(batch, ext_rows, D)], axis=2
    )
    count = lax.axis_size("seq")
    forward = [(i, i + 1) for i in range(count - 1)]
    backward = [(target, source) for source, target in forward]
    from_high = lax.ppermute(grad_kv_ext[:, :HALF].astype(jnp.bfloat16), "seq", backward)
    from_low = lax.ppermute(grad_kv_ext[:, HALF + tokens :].astype(jnp.bfloat16), "seq", forward)
    rest = ((0, 0), (0, tokens - HALF), (0, 0))
    own_rows = grad_kv_ext[:, HALF : HALF + tokens]
    own_rows = own_rows + jnp.pad(from_low.astype(jnp.float32), rest)
    own_rows = own_rows + jnp.pad(from_high.astype(jnp.float32), (rest[0], rest[1][::-1], rest[2]))
    grad_k = rotate_back(own_rows[..., :D].reshape(head_shape), cosine, sine_table)
    grad_q = rotate_back(grad_q, cosine, sine_table)
    flat = batch * tokens
    grad_qkv = jnp.concatenate(
        [grad_q.reshape(flat, D), grad_k.reshape(flat, D), own_rows[..., D:].reshape(flat, D)],
        axis=1,
    ).astype(jnp.bfloat16)
    grad_wqkv = weight_grad(a_low, grad_qkv, core)
    grad_a = jnp.einsum("te,de->td", grad_qkv, w_mix[:, : 3 * D], preferred_element_type=jnp.float32)
    normed_a, inverse_a = norm_forward(hidden)
    grad_in_part, grad_gain_attn = norm_backward(grad_a, normed_a, inverse_a, gain_attn)
    return (grad_middle + grad_in_part, (grad_wqkv, grad_w_out, grad_gain_attn))


def owner_batches(own, other, core):
    mine = jnp.where(core == 0, own, other)
    received = swap_cores(jnp.where(core == 0, other, own))
    first = core == 0
    return jnp.concatenate(
        [jnp.where(first, mine, received), jnp.where(first, received, mine)], axis=0
    )


def local(
    inputs,
    cotangent,
    doc_lengths,
    qkv_weight,
    out_weight,
    attn_gain,
    wide_weight,
    narrow_weight,
    mlp_gain,
):
    core = lax.axis_index("section")
    seq_num = lax.axis_index("seq")
    share = inputs.shape[0] // 2
    tokens_here = inputs.shape[2]
    total_len = tokens_here * lax.axis_size("seq")

    gains = jnp.stack([attn_gain[0], mlp_gain[0]], axis=1)
    gains = jnp.pad(gains, ((0, 0), (0, 126)))
    mix = own_halves(jnp.concatenate([qkv_weight[0], out_weight[0], gains], axis=1), core)
    mlp = own_halves(jnp.concatenate([wide_weight[0], narrow_weight[0]], axis=1), core)
    params = []
    before = None
    for layer in range(2):
        gathered = []
        for half in (mix[layer], mlp[layer]):
            if before is not None:
                half, before = lax.optimization_barrier((half, before))
            before = along_seq(half)
            gathered.append(gather_rest(before, core))
        gain_rows = gathered[0][:, 4 * D : 4 * D + 2].astype(jnp.float32).T
        params.append((gathered[0], gathered[1], gain_rows[0], gain_rows[1]))

    half_dim = HEAD_DIM // 2
    frequency = jnp.power(theta_base, jnp.arange(half_dim).astype(jnp.float32) * (-2.0 / HEAD_DIM))
    positions = (seq_num * tokens_here + jnp.arange(tokens_here, dtype=jnp.int32)).astype(
        jnp.float32
    )
    angles = positions[:, None] * frequency[None, :]
    cosine = jnp.cos(angles)[None, :, None, :]
    sine_table = jnp.sin(angles)[None, :, None, :]

    def mine(values):
        return lax.dynamic_slice_in_dim(values[:, 0], core * share, share, 0)

    lengths = mine(doc_lengths)
    allowed = jnp.stack(
        [make_tables(lengths[i], seq_num, tokens_here, total_len) for i in range(share)]
    )
    flat = share * tokens_here
    hidden = mine(inputs).reshape(flat, D).astype(jnp.float32)
    saves, outputs = [], []
    for layer in range(2):
        output, saved = forward_layer(hidden, params[layer], allowed, cosine, sine_table)
        saves.append(saved)
        outputs.append(output.astype(jnp.bfloat16))
        hidden = outputs[-1].astype(jnp.float32)
    grad_out = mine(cotangent).reshape(flat, D).astype(jnp.float32)
    parts, grads_in = [None, None], [None, None]
    for layer in (1, 0):
        grad_middle, mlp_part = backward_mlp(grad_out, saves[layer], params[layer], core)
        grads_in[layer], attn_part = backward_attn(
            grad_middle, saves[layer], params[layer], core, cosine, sine_table
        )
        parts[layer] = attn_part + mlp_part
        grad_out = grads_in[layer].astype(jnp.bfloat16).astype(jnp.float32)

    def rows_of(number):
        return owner_rows([parts[0][number], parts[1][number]], core)[None]

    gain_sums = sum_everywhere(
        jnp.stack([parts[layer][number] for layer in range(2) for number in (2, 5)])
    )
    rows = qkv_weight.shape[1]
    start = (seq_num * lax.axis_size("fsdp") + lax.axis_index("fsdp")) * rows
    gain_sums = lax.dynamic_slice(gain_sums, (core * 2, start), (2, rows))
    shape = (share, tokens_here, D)
    activations = owner_batches(outputs[0].reshape(shape), outputs[1].reshape(shape), core)
    input_grads = owner_batches(grads_in[0].reshape(shape), grads_in[1].reshape(shape), core)
    return (
        activations[None, :, None],
        input_grads[None, :, None],
        rows_of(0),
        rows_of(1),
        gain_sums[:1],
        rows_of(3),
        rows_of(4),
        gain_sums[1:],
    )


def solution(mesh):
    placed = (
        P(None, "fsdp", "seq", None),
        P(None, "fsdp", "seq", None),
        P(None, "fsdp", None),
        P("section", ("seq", "fsdp"), None),
        P("section", ("seq", "fsdp"), None),
        P("section", ("seq", "fsdp")),
        P("section", ("seq", "fsdp"), None),
        P("section", ("seq", "fsdp"), None),
        P("section", ("seq", "fsdp")),
    )
    return jax.shard_map(
        local,
        mesh=mesh,
        in_specs=placed,
        out_specs=(
            P("section", None, "fsdp", "seq", None),
            P("section", None, "fsdp", "seq", None),
            P("section", ("seq", "fsdp"), None),
            P("section", ("seq", "fsdp"), None),
            P("section", ("seq", "fsdp")),
            P("section", ("seq", "fsdp"), None),
            P("section", ("seq", "fsdp"), None),
            P("section", ("seq", "fsdp")),
        ),
        check_vma=False,
    )
```

```python
import math

import jax
import jax.numpy as jnp
from jax import lax
from jax.experimental.layout import Layout, with_layout_constraint
from jax.sharding import PartitionSpec as P

D = 1024
FF = 2624
HEADS = 16
HEAD_DIM = 64
HALF = 64


eps_norm = 1e-05
theta_base = 10000.0
masked_fill = -1e30


def norm_forward(values):
    center = jnp.mean(values, axis=-1, keepdims=True)
    shifted = values - center
    spread = jnp.mean(shifted * shifted, axis=-1, keepdims=True)
    inverse = lax.rsqrt(spread + eps_norm)
    return (shifted * inverse, inverse)


def norm_backward(grad_out, normed, inverse, gain):
    scaled = grad_out * gain
    gain_grad = jnp.sum(grad_out * normed, axis=0)
    first_mean = jnp.mean(scaled, axis=-1, keepdims=True)
    second_mean = jnp.mean(scaled * normed, axis=-1, keepdims=True)
    return (inverse * (scaled - first_mean - normed * second_mean), gain_grad)


def rotate(values, cosine, sine_table):
    half_dim = values.shape[-1] // 2
    first_half = values[..., :half_dim]
    second_half = values[..., half_dim:]
    return jnp.concatenate(
        [
            first_half * cosine - second_half * sine_table,
            second_half * cosine + first_half * sine_table,
        ],
        axis=-1,
    )


def rotate_back(grads, cosine, sine_table):
    half_dim = grads.shape[-1] // 2
    first_half = grads[..., :half_dim]
    second_half = grads[..., half_dim:]
    return jnp.concatenate(
        [
            first_half * cosine + second_half * sine_table,
            second_half * cosine - first_half * sine_table,
        ],
        axis=-1,
    )


def gelu_slope(values):
    normal_cdf = 0.5 * (1.0 + jax.scipy.special.erf(values * 2.0 ** (-0.5)))
    return normal_cdf + values * jnp.exp(-0.5 * values * values) * (2.0 * math.pi) ** (-0.5)


def make_tables(lengths_row, seq_num, tokens_here, total_len):
    ends = jnp.cumsum(lengths_row)
    spots = seq_num * tokens_here - HALF + jnp.arange(tokens_here + 2 * HALF, dtype=jnp.int32)
    doc_ext = jnp.sum((ends[None, :] <= spots[:, None]).astype(jnp.int32), axis=1)
    inside = (spots >= 0) & (spots < total_len)
    doc_rows = doc_ext[HALF : HALF + tokens_here]
    nearby = (
        jnp.abs(
            jnp.arange(tokens_here)[:, None] - jnp.arange(tokens_here + 2 * HALF)[None, :] + HALF
        )
        <= HALF
    )
    return nearby & inside[None, :] & (doc_rows[:, None] == doc_ext[None, :])


def flip_pairs(order, spots):
    pairs = []
    for section in range(2):
        bit = (1, 2)[(section + order) % 2]
        pairs += [(section * spots + spot, section * spots + (spot ^ bit)) for spot in range(spots)]
    return pairs


def flip(x, order):
    return lax.ppermute(x, ("section", "fsdp"), flip_pairs(order, lax.axis_size("fsdp")))


def swap_cores(x):
    return lax.ppermute(x, "section", [(0, 1), (1, 0)])


def shift_seq(x, by):
    count = lax.axis_size("seq")
    return lax.ppermute(x, "seq", [(i, (i + by) % count) for i in range(count)])


def halo(block, width):
    count = lax.axis_size("seq")
    forward = [(i, i + 1) for i in range(count - 1)]
    backward = [(target, source) for source, target in forward]
    low = lax.ppermute(block[:, block.shape[1] - width :], "seq", forward)
    high = lax.ppermute(block[:, :width], "seq", backward)
    return low, high


def own_halves(shard, core):
    rows = shard.shape[0] // 2
    mine = lax.dynamic_slice_in_dim(shard, core * rows, rows, 0)
    received = swap_cores(lax.dynamic_slice_in_dim(shard, (1 - core) * rows, rows, 0))
    return [jnp.where(core == layer, mine, received) for layer in range(2)]


def after(*values):
    total = 0.0
    for value in values:
        total = total + value[(0,) * value.ndim].astype(jnp.float32) * 0.0
    return total


def along_seq(half, tie):
    count, place = lax.axis_size("seq"), lax.axis_index("seq")
    pieces = [shift_seq(half, by) for by in range(1, count)]
    place = place + tie.astype(jnp.int32)
    out = jnp.zeros((count,) + half.shape, half.dtype)
    out = lax.dynamic_update_slice(out, half[None], (place, 0, 0))
    for by, piece in enumerate(pieces, 1):
        out = lax.dynamic_update_slice(out, piece[None], ((place - by) % count, 0, 0))
    return out


def spread(column):
    one, two = flip(column, 0), flip(column, 1)
    three = flip(one, 1)
    pieces = (column, one, two, three)
    return pieces, tuple(swap_cores(piece) for piece in pieces)


def assemble(pieces, core, tie):
    spots, spot = lax.axis_size("fsdp"), lax.axis_index("fsdp")
    seq_count, rows, columns = pieces[0][0].shape
    first_bit = jnp.where(core == 0, 1, 2)
    core = core + tie.astype(jnp.int32)
    full = jnp.zeros((seq_count, spots * 2, rows, columns), pieces[0][0].dtype)
    places = (spot, spot ^ first_bit, spot ^ (3 - first_bit), spot ^ 3)
    swapped = (places[0], places[2], places[1], places[3])
    for mine, place, theirs, other in zip(pieces[0], places, pieces[1], swapped):
        full = lax.dynamic_update_slice(full, mine[:, None], (0, place * 2 + core, 0, 0))
        full = lax.dynamic_update_slice(full, theirs[:, None], (0, other * 2 + 1 - core, 0, 0))
    return full.reshape(seq_count * spots * 2 * rows, columns)


class WeightGrad:
    def __init__(self, left, right, core):
        seq_count, spots, spot = lax.axis_size("seq"), lax.axis_size("fsdp"), lax.axis_index("fsdp")
        tokens, width = left.shape
        columns = right.shape[1]
        rows = width // (seq_count * spots * 2)
        first_bit = jnp.where(core == 0, 1, 2)
        other_bit = 3 - first_bit
        turned = left.T.reshape(seq_count, spots * 2, rows, tokens)

        def product(places, half):
            chosen = [lax.dynamic_slice_in_dim(turned, p * 2 + half, 1, 1)[:, 0] for p in places]
            chosen = jnp.stack(chosen).reshape(len(places) * seq_count * rows, tokens)
            out = jnp.dot(chosen, right, preferred_element_type=jnp.float32).astype(jnp.bfloat16)
            out = with_layout_constraint(out, Layout(major_to_minor=(0, 1)))
            return out.reshape(len(places), seq_count, rows, columns)

        self.out = [
            product((spot ^ other_bit, spot ^ 3), 1 - core),
            product((spot, spot ^ first_bit), 1 - core),
            product((spot ^ first_bit, spot ^ 3), core),
            product((spot, spot ^ other_bit), core),
        ]

    def products(self):
        self.sent, self.kept = swap_cores(self.out[0]), swap_cores(self.out[1])
        return after(*self.out)

    def first(self):
        value = (widen(self.out[2]) + widen(self.sent)).astype(jnp.bfloat16)
        self.one = flip(value, 0)
        return after(value)

    def second(self):
        base = widen(self.out[3]) + widen(self.kept)
        value = (base[1] + widen(self.one[1])).astype(jnp.bfloat16)
        self.two = flip(value, 1)
        return after(value)

    def third(self):
        base = widen(self.out[3][0]) + widen(self.kept[0])
        mine = (base + widen(self.one[0]) + widen(self.two)).astype(jnp.bfloat16)
        count, place = lax.axis_size("seq"), lax.axis_index("seq")
        own = lax.dynamic_index_in_dim(mine, place, 0, keepdims=False)
        self.total = widen(own)
        for by in range(1, count):
            out = lax.dynamic_index_in_dim(mine, (place + by) % count, 0, keepdims=False)
            self.total = self.total + widen(shift_seq(out, by))
        return after(mine)


def widen(value):
    return value.astype(jnp.float32)


def owner_rows(pieces, core):
    mine = jnp.where(core == 0, pieces[0], pieces[1])
    received = swap_cores(jnp.where(core == 0, pieces[1], pieces[0]))
    first = core == 0
    return jnp.concatenate(
        [jnp.where(first, mine, received), jnp.where(first, received, mine)], axis=0
    )


def sum_everywhere(x):
    x = x + swap_cores(x)
    x = x + flip(x, 0)
    x = x + flip(x, 1)
    return x + sum(shift_seq(x, by) for by in range(1, lax.axis_size("seq")))


def forward_attn(hidden, w_mix, gain_attn, allowed, cosine, sine_table):
    batch, tokens = allowed.shape[:2]
    score_scale = HEAD_DIM ** (-0.5)
    normed_a, inverse_a = norm_forward(hidden)
    a_low = (normed_a * gain_attn).astype(jnp.bfloat16)
    mixed = jnp.dot(a_low, w_mix[:, : 3 * D], preferred_element_type=jnp.float32)
    head_shape = (batch, tokens, HEADS, HEAD_DIM)
    queries = rotate(mixed[:, :D].reshape(head_shape), cosine, sine_table).astype(jnp.bfloat16)
    keys = rotate(mixed[:, D : 2 * D].reshape(head_shape), cosine, sine_table).astype(jnp.bfloat16)
    values = mixed[:, 2 * D :].astype(jnp.bfloat16)
    key_value = jnp.concatenate(
        [keys.reshape(batch, tokens, D), values.reshape(batch, tokens, D)], axis=2
    )
    low, high = halo(key_value, HALF)
    kv_ext = jnp.concatenate([low, key_value, high], axis=1)
    ext_shape = (batch, tokens + 2 * HALF, HEADS, HEAD_DIM)
    k_ext = kv_ext[..., :D].reshape(ext_shape)
    v_ext = kv_ext[..., D:].reshape(ext_shape)
    scores = (
        jnp.einsum("bqhd,bkhd->bhqk", queries, k_ext, preferred_element_type=jnp.float32)
        * score_scale
    )
    scores = jnp.where(allowed[:, None], scores, masked_fill)
    row_peak = jnp.max(scores, axis=-1, keepdims=True)
    exp_scores = jnp.exp(scores - row_peak)
    softmax_prob = exp_scores / jnp.sum(exp_scores, axis=-1, keepdims=True)
    attended = jnp.einsum(
        "bhqk,bkhd->bqhd",
        softmax_prob.astype(jnp.bfloat16),
        v_ext,
        preferred_element_type=jnp.float32,
    )
    o_low = attended.reshape(batch * tokens, D).astype(jnp.bfloat16)
    middle = hidden + jnp.dot(o_low, w_mix[:, 3 * D : 4 * D], preferred_element_type=jnp.float32)
    return middle, (hidden, a_low, queries, k_ext, v_ext, softmax_prob, o_low)


def forward_mlp(middle, w_mlp, gain_mlp):
    normed_b, inverse_b = norm_forward(middle)
    b_low = (normed_b * gain_mlp).astype(jnp.bfloat16)
    wide = jnp.dot(b_low, w_mlp[:, : 2 * FF], preferred_element_type=jnp.float32)
    m_low = (jax.nn.gelu(wide[:, :FF], approximate=False) * wide[:, FF:]).astype(jnp.bfloat16)
    output = middle + jnp.einsum(
        "tf,df->td", m_low, w_mlp[:, 2 * FF :], preferred_element_type=jnp.float32
    )
    return output, (middle, b_low, wide, m_low)


def backward_mlp(grad_out, saved, params, core, steps):
    w_mix, w_mlp, gain_attn, gain_mlp = params
    hidden, a_low, queries, k_ext, v_ext, softmax_prob, o_low, middle, b_low, wide, m_low = saved
    g_mlp = grad_out.astype(jnp.bfloat16)
    narrow = WeightGrad(g_mlp, m_low, core)
    grad_m = jnp.dot(g_mlp, w_mlp[:, 2 * FF :], preferred_element_type=jnp.float32)
    grad_m = grad_m + (narrow.products() + steps["grad_m"]())
    gelu_input = wide[:, :FF]
    gate_part = wide[:, FF:]
    activated = jax.nn.gelu(gelu_input, approximate=False)
    grad_wide = jnp.concatenate(
        [grad_m * gate_part * gelu_slope(gelu_input), grad_m * activated], axis=1
    ).astype(jnp.bfloat16)
    in_wide = WeightGrad(b_low, grad_wide, core)
    grad_b = jnp.einsum(
        "tf,df->td", grad_wide, w_mlp[:, : 2 * FF], preferred_element_type=jnp.float32
    )
    normed_b, inverse_b = norm_forward(middle)
    inverse_b = inverse_b + (in_wide.products() + narrow.first() + steps["norm_b"]())
    grad_mid_part, grad_gain_mlp = norm_backward(grad_b, normed_b, inverse_b, gain_mlp)
    return (grad_out + grad_mid_part, (in_wide, narrow, grad_gain_mlp))


def backward_attn(grad_middle, saved, params, core, cosine, sine_table, steps):
    w_mix, w_mlp, gain_attn, gain_mlp = params
    hidden, a_low, queries, k_ext, v_ext, softmax_prob, o_low, middle, b_low, wide, m_low = saved
    batch, tokens = queries.shape[:2]
    ext_rows = k_ext.shape[1]
    score_scale = HEAD_DIM ** (-0.5)
    g_attn = grad_middle.astype(jnp.bfloat16)
    out_grad = WeightGrad(o_low, g_attn, core)
    grad_o = jnp.einsum(
        "te,de->td", g_attn, w_mix[:, 3 * D : 4 * D], preferred_element_type=jnp.float32
    ).astype(jnp.bfloat16)
    head_shape = (batch, tokens, HEADS, HEAD_DIM)
    grad_o = grad_o.reshape(head_shape)
    grad_prob = jnp.einsum("bqhd,bkhd->bhqk", grad_o, v_ext, preferred_element_type=jnp.float32)
    grad_v_ext = jnp.einsum(
        "bhqk,bqhd->bkhd",
        softmax_prob.astype(jnp.bfloat16),
        grad_o,
        preferred_element_type=jnp.float32,
    )
    row_delta = jnp.sum(softmax_prob * grad_prob, axis=-1, keepdims=True)
    row_delta = row_delta + (out_grad.products() + steps["delta"]())
    grad_scores = (softmax_prob * (grad_prob - row_delta)).astype(jnp.bfloat16)
    grad_q = (
        jnp.einsum("bhqk,bkhd->bqhd", grad_scores, k_ext, preferred_element_type=jnp.float32)
        * score_scale
    )
    grad_k_ext = (
        jnp.einsum("bhqk,bqhd->bkhd", grad_scores, queries, preferred_element_type=jnp.float32)
        * score_scale
    )
    grad_kv_ext = jnp.concatenate(
        [grad_k_ext.reshape(batch, ext_rows, D), grad_v_ext.reshape(batch, ext_rows, D)], axis=2
    )
    count = lax.axis_size("seq")
    forward = [(i, i + 1) for i in range(count - 1)]
    backward = [(target, source) for source, target in forward]
    from_high = lax.ppermute(grad_kv_ext[:, :HALF].astype(jnp.bfloat16), "seq", backward)
    from_low = lax.ppermute(grad_kv_ext[:, HALF + tokens :].astype(jnp.bfloat16), "seq", forward)
    rest = ((0, 0), (0, tokens - HALF), (0, 0))
    own_rows = grad_kv_ext[:, HALF : HALF + tokens]
    own_rows = own_rows + jnp.pad(from_low.astype(jnp.float32), rest)
    own_rows = own_rows + jnp.pad(from_high.astype(jnp.float32), (rest[0], rest[1][::-1], rest[2]))
    tie = out_grad.first() + steps["rotate"]()
    cosine, sine_table = cosine + tie, sine_table + tie
    grad_k = rotate_back(own_rows[..., :D].reshape(head_shape), cosine, sine_table)
    grad_q = rotate_back(grad_q, cosine, sine_table)
    flat = batch * tokens
    grad_qkv = jnp.concatenate(
        [grad_q.reshape(flat, D), grad_k.reshape(flat, D), own_rows[..., D:].reshape(flat, D)],
        axis=1,
    ).astype(jnp.bfloat16)
    qkv_grad = WeightGrad(a_low, grad_qkv, core)
    grad_a = jnp.einsum("te,de->td", grad_qkv, w_mix[:, : 3 * D], preferred_element_type=jnp.float32)
    normed_a, inverse_a = norm_forward(hidden)
    inverse_a = inverse_a + (qkv_grad.products() + steps["norm_a"]())
    grad_in_part, grad_gain_attn = norm_backward(grad_a, normed_a, inverse_a, gain_attn)
    return (grad_middle + grad_in_part, (qkv_grad, out_grad, grad_gain_attn))


def owner_batches(own, other, core):
    mine = jnp.where(core == 0, own, other)
    received = swap_cores(jnp.where(core == 0, other, own))
    first = core == 0
    return jnp.concatenate(
        [jnp.where(first, mine, received), jnp.where(first, received, mine)], axis=0
    )


def local(
    inputs,
    cotangent,
    doc_lengths,
    qkv_weight,
    out_weight,
    attn_gain,
    wide_weight,
    narrow_weight,
    mlp_gain,
):
    core = lax.axis_index("section")
    seq_num = lax.axis_index("seq")
    share = inputs.shape[0] // 2
    tokens_here = inputs.shape[2]
    total_len = tokens_here * lax.axis_size("seq")

    gains = jnp.stack([attn_gain[0], mlp_gain[0]], axis=1)
    gains = jnp.pad(gains, ((0, 0), (0, 126)))
    mix = own_halves(jnp.concatenate([qkv_weight[0], out_weight[0], gains], axis=1), core)
    mlp = own_halves(jnp.concatenate([wide_weight[0], narrow_weight[0]], axis=1), core)
    halves = (mix[0], mlp[0], mix[1], mlp[1])
    columns, pieces = [], []
    for number, half in enumerate(halves):
        tie = after(pieces[-1][0][1]) if number > 0 else after(half)
        if number > 0:
            half = half + after(columns[-1]).astype(half.dtype)
        columns.append(along_seq(half, tie))
        pieces.append(spread(columns[-1]))

    half_dim = HEAD_DIM // 2
    frequency = jnp.power(theta_base, jnp.arange(half_dim).astype(jnp.float32) * (-2.0 / HEAD_DIM))
    positions = (seq_num * tokens_here + jnp.arange(tokens_here, dtype=jnp.int32)).astype(
        jnp.float32
    )
    angles = positions[:, None] * frequency[None, :]
    cosine = jnp.cos(angles)[None, :, None, :]
    sine_table = jnp.sin(angles)[None, :, None, :]

    def mine(values):
        return lax.dynamic_slice_in_dim(values[:, 0], core * share, share, 0)

    lengths = mine(doc_lengths)
    allowed = jnp.stack(
        [make_tables(lengths[i], seq_num, tokens_here, total_len) for i in range(share)]
    )
    flat = share * tokens_here
    hidden = mine(inputs).reshape(flat, D).astype(jnp.float32)
    params, saves, outputs = [], [], []
    tie = after(hidden)
    for layer in range(2):
        w_mix = assemble(pieces[2 * layer], core, tie)
        gain_rows = w_mix[:, 4 * D : 4 * D + 2].astype(jnp.float32).T
        middle, saved_attn = forward_attn(
            hidden, w_mix, gain_rows[0], allowed, cosine, sine_table
        )
        w_mlp = assemble(pieces[2 * layer + 1], core, after(middle))
        params.append((w_mix, w_mlp, gain_rows[0], gain_rows[1]))
        output, saved_mlp = forward_mlp(middle, w_mlp, gain_rows[1])
        saves.append(saved_attn + saved_mlp)
        outputs.append(output.astype(jnp.bfloat16))
        hidden = outputs[-1].astype(jnp.float32)
        tie = after(saved_mlp[2])
    grad_out = mine(cotangent).reshape(flat, D).astype(jnp.float32)
    parts, grads_in = [None, None], [None, None]
    nothing = lambda: 0.0
    previous = None
    for layer in (1, 0):
        if previous is None:
            steps = dict.fromkeys(("grad_m", "norm_b", "delta", "rotate", "norm_a"), nothing)
        else:
            qkv, out, _, wide, narrow, _ = previous
            steps = {
                "grad_m": lambda: qkv.first() + wide.second(),
                "norm_b": lambda: out.second() + narrow.third(),
                "delta": lambda: qkv.second() + wide.third(),
                "rotate": lambda: out.third(),
                "norm_a": lambda: qkv.third(),
            }
        grad_middle, mlp_part = backward_mlp(grad_out, saves[layer], params[layer], core, steps)
        wide_now, narrow_now = mlp_part[0], mlp_part[1]
        ahead = dict(steps)
        ahead["delta"] = lambda: wide_now.first() + steps["delta"]()
        ahead["rotate"] = lambda: narrow_now.second() + steps["rotate"]()
        grads_in[layer], attn_part = backward_attn(
            grad_middle, saves[layer], params[layer], core, cosine, sine_table, ahead
        )
        parts[layer] = attn_part + mlp_part
        previous = parts[layer]
        grad_out = grads_in[layer].astype(jnp.bfloat16).astype(jnp.float32)
    qkv, out, _, wide, narrow, _ = previous
    for last_step in (wide.second, qkv.first, narrow.third, out.second, wide.third, qkv.second):
        last_step()
    out.third()
    qkv.third()

    def rows_of(number):
        return owner_rows([parts[0][number].total, parts[1][number].total], core)[None]

    gain_sums = sum_everywhere(
        jnp.stack([parts[layer][number] for layer in range(2) for number in (2, 5)])
    )
    rows = qkv_weight.shape[1]
    start = (seq_num * lax.axis_size("fsdp") + lax.axis_index("fsdp")) * rows
    gain_sums = lax.dynamic_slice(gain_sums, (core * 2, start), (2, rows))
    shape = (share, tokens_here, D)
    activations = owner_batches(outputs[0].reshape(shape), outputs[1].reshape(shape), core)
    input_grads = owner_batches(grads_in[0].reshape(shape), grads_in[1].reshape(shape), core)
    return (
        activations[None, :, None],
        input_grads[None, :, None],
        rows_of(0),
        rows_of(1),
        gain_sums[:1],
        rows_of(3),
        rows_of(4),
        gain_sums[1:],
    )


def solution(mesh):
    placed = (
        P(None, "fsdp", "seq", None),
        P(None, "fsdp", "seq", None),
        P(None, "fsdp", None),
        P("section", ("seq", "fsdp"), None),
        P("section", ("seq", "fsdp"), None),
        P("section", ("seq", "fsdp")),
        P("section", ("seq", "fsdp"), None),
        P("section", ("seq", "fsdp"), None),
        P("section", ("seq", "fsdp")),
    )
    return jax.shard_map(
        local,
        mesh=mesh,
        in_specs=placed,
        out_specs=(
            P("section", None, "fsdp", "seq", None),
            P("section", None, "fsdp", "seq", None),
            P("section", ("seq", "fsdp"), None),
            P("section", ("seq", "fsdp"), None),
            P("section", ("seq", "fsdp")),
            P("section", ("seq", "fsdp"), None),
            P("section", ("seq", "fsdp"), None),
            P("section", ("seq", "fsdp")),
        ),
        check_vma=False,
    )
```
